512 devices in a mesh: row: 32 (over x, y, core), col: 16 (over z).
Axes of the slice: x: 4, y: 4, z: 16, core: 2. Of those that a mesh axis runs over, the one named last changes fastest.
Arguments:
- diag_blocks: bfloat16 [4096, 128, 128], P(('row', 'col')), may hold values from -0.03 to 3, as said below
- off_blocks: bfloat16 [4096, 6, 128, 128], P(('row', 'col')), may hold values from -0.375 to 0.375
- neighbors: int32 [4096, 6], P(('row', 'col')), may hold values from -1 to 4095, as said below
- levels: int32 [4096], P(('row', 'col')), may hold values from 0 to 1, as said below
Outputs:
- pivot_inverse: bfloat16 [4096, 128, 128], P(('row', 'col'))
- factor_blocks: bfloat16 [4096, 6, 128, 128], P(('row', 'col'))
The draws below stay inside these ranges and needn't reach their ends.
Inputs may be any that keep to these rules, and one draw needn't show every extreme that they name: `levels`: block row i lies on device number d = i // 8, where d = r * (number of devices along col) + c for the device with index r along row and index c along col. On each device the rows of level 0 come first; a device holds between 2 and 6 rows of level 0, and in every draw some device holds exactly 6 and some exactly 2. `neighbors`: A live slot names a row of the other level. Slot 0 names a row on the device whose row index is one higher, slot 1 one lower, slot 2 on the device whose col index is one higher, slot 3 one lower, slots 4 and 5 on the same device. If row i names row j in slot k, row j names row i in slot (1, 0, 3, 2, 5, 4)[k]. `diag_blocks`: diagonal entries from 1 to 3; off-diagonal entries of either sign, each row's sum of their magnitudes under 0.9 times that row's diagonal entry.
All inputs are finite; a program needn't handle non-finite values.
Results may differ from the reference program's by a relative error of at most 0.0053.
Values may be sent and summed in bfloat16 or wider, within the bound.
A program may use at most 64 MiB of HBM per device.

```python
import math
import jax
import jax.numpy as jnp
import numpy as np
from jax import lax

B = 128
K = 6
NB = 8
NS_STEPS = 4
CAP = 6
NROWS = 4096
N_ROW = 32
N_COL = 16


MOVES = ((1, 0), (-1, 0), (0, 1), (0, -1), (0, 0), (0, 0))


def slot_pattern(key):
    base = jax.random.fold_in(key, 913)
    count_key, pick_key, shift_key = jax.random.split(base, 3)
    devices_all = N_ROW * N_COL
    lowest = NB - CAP
    counts = jax.random.randint(count_key, (devices_all,), lowest, CAP + 1)
    chosen = jax.random.permutation(pick_key, devices_all)
    counts = counts.at[chosen[0]].set(CAP).at[chosen[1]].set(lowest)
    shifts = jax.random.randint(shift_key, (K, devices_all), 0, 3)
    device = jnp.arange(devices_all, dtype=jnp.int32)[:, None]
    position = jnp.arange(NB, dtype=jnp.int32)[None, :]
    early_count = counts[:, None]
    level_table = (position >= early_count).astype(jnp.int32)
    grid_row = device // N_COL
    grid_col = device % N_COL
    columns = []
    for slot_index in range(K):
        step_row, step_col = MOVES[slot_index]
        target_row = grid_row + step_row
        target_col = grid_col + step_col
        inside = (target_row >= 0) & (target_row < N_ROW) & (target_col >= 0) & (target_col < N_COL)
        target = jnp.clip(target_row, 0, N_ROW - 1) * N_COL + jnp.clip(target_col, 0, N_COL - 1)
        target_count = counts[target]
        late_rank = position - early_count + shifts[slot_index][device]
        late_ok = inside & (late_rank < target_count)
        late_value = target * NB + late_rank
        early_rank = position - shifts[slot_index ^ 1][target]
        early_ok = inside & (early_rank >= 0) & (early_rank < NB - target_count)
        early_value = target * NB + target_count + early_rank
        value = jnp.where(level_table == 1, jnp.where(late_ok, late_value, -1), jnp.where(early_ok, early_value, -1))
        columns.append(value)
    named = jnp.stack(columns, axis=-1).reshape(NROWS, K).astype(jnp.int32)
    return (level_table.reshape(NROWS).astype(jnp.int32), named)


def draw_levels(key, part):
    return slot_pattern(key)[0]


def draw_neighbors(key, part):
    return slot_pattern(key)[1]


def draw_diag_blocks(key, part):
    scale_key, spread_key, sign_key = jax.random.split(jax.random.fold_in(key, 5), 3)
    diagonal = jnp.exp(jax.random.uniform(scale_key, (NROWS, B), minval=0.0, maxval=math.log(3.0)))
    spread = jax.random.uniform(spread_key, (NROWS, B, B), minval=0.4, maxval=1.0)
    signs = jnp.where(jax.random.uniform(sign_key, (NROWS, B, B)) < 0.5, -1.0, 1.0)
    identity = jnp.eye(B, dtype=jnp.float32)
    denominator = max(B, 128) - 1
    coupling = diagonal[:, :, None] * signs * spread * (0.85 / denominator)
    matrix = coupling * (1.0 - identity) + diagonal[:, :, None] * identity
    return matrix.astype(jnp.bfloat16)


def level_of(key, extent, pieces, low, largest):
    gain = 1.0
    for dim, parts in pieces:
        heights = jax.random.uniform(jax.random.fold_in(jax.random.fold_in(key, 6), dim), (parts,), jnp.float32, low / len(pieces), largest / len(pieces))
        gain = gain * jnp.repeat(jnp.exp(heights), extent[dim] // parts).reshape((-1,) + (1,) * (len(extent) - 1 - dim))
    return gain


def normal_values(rng, shape, scale, bound, cuts=(), kind=jnp.bfloat16):
    values = jax.random.normal(rng, shape, jnp.float32) * scale
    if len(cuts) > 0:
        values = level_of(rng, shape, cuts, -0.22, 0.18) * values
    return jnp.clip(values, min=-bound, max=bound).astype(kind)


def setup_inputs(seed: int = 0) -> dict:
    splits = jax.random.split(jax.random.key(seed), 5)
    diag_blocks = draw_diag_blocks(jax.random.fold_in(splits[4], 71), 0)
    off_blocks = normal_values(splits[1], (NROWS, K, B, B), 0.025, 0.375, ((0, 512),))
    neighbors = draw_neighbors(jax.random.fold_in(splits[4], 71), 0)
    levels = draw_levels(jax.random.fold_in(splits[4], 71), 0)
    return dict(diag_blocks=diag_blocks, off_blocks=off_blocks, neighbors=neighbors, levels=levels)


MIRROR_TABLE = np.array([1, 0, 3, 2, 5, 4], dtype=np.int32)


def approx_inverse(matrix):
    magnitude = jnp.abs(matrix)
    column_norm = jnp.max(jnp.sum(magnitude, axis=1), axis=1)
    row_norm = jnp.max(jnp.sum(magnitude, axis=2), axis=1)
    iterate = jnp.swapaxes(matrix, 1, 2) / (column_norm * row_norm)[:, None, None]
    for step_index in range(NS_STEPS):
        product = jnp.einsum('nij,njk->nik', matrix, iterate, precision=lax.Precision.HIGHEST)
        iterate = 2.0 * iterate - jnp.einsum('nij,njk->nik', iterate, product, precision=lax.Precision.HIGHEST)
    return iterate


def reference(diag_blocks, off_blocks, neighbors, levels):
    groups = NROWS // NB
    active = neighbors >= 0

    def first_pass(items):
        diag_group, off_group, active_group = items
        inverse = approx_inverse(diag_group.astype(jnp.float32)).astype(jnp.bfloat16)
        scaled = jnp.einsum('nij,nkjl->nkil', inverse.astype(jnp.float32), off_group.astype(jnp.float32))
        scaled = jnp.where(active_group[:, :, None, None], scaled, 0.0).astype(jnp.bfloat16)
        return inverse, scaled

    inverses, scaled_rows = lax.map(first_pass, (diag_blocks.reshape(groups, NB, B, B), off_blocks.reshape(groups, NB, K, B, B), active.reshape(groups, NB, K)))
    inverses = inverses.reshape(NROWS, B, B)
    scaled_rows = scaled_rows.reshape(NROWS, K, B, B)
    mirror = jnp.asarray(MIRROR_TABLE)

    def second_pass(items):
        diag_group, off_group, named_group, level_group = items
        active_group = named_group >= 0
        target = jnp.where(active_group, named_group, 0).astype(jnp.int32)
        across = inverses[target].astype(jnp.float32)
        facing = scaled_rows[target, mirror[None, :]].astype(jnp.float32)
        lower_blocks = jnp.where(active_group[:, :, None, None], off_group.astype(jnp.float32), 0.0)
        lower_factor = jnp.einsum('qkij,qkjl->qkil', lower_blocks, across).astype(jnp.bfloat16)
        schur = jnp.einsum('qkij,qkjl->qil', lower_blocks, facing)
        diag_float = diag_group.astype(jnp.float32)
        later = (level_group == 1)[:, None, None]
        pivot = jnp.where(later, diag_float - schur, diag_float)
        return approx_inverse(pivot).astype(jnp.bfloat16), lower_factor

    pivots, lowers = lax.map(second_pass, (diag_blocks.reshape(groups, NB, B, B), off_blocks.reshape(groups, NB, K, B, B), neighbors.reshape(groups, NB, K), levels.reshape(groups, NB)))
    lowers = lowers.reshape(NROWS, K, B, B)
    factor = jnp.where((levels == 0)[:, None, None, None], scaled_rows, lowers)
    return pivots.reshape(NROWS, B, B), factor
```

```python
import jax
import jax.numpy as jnp
from jax import lax
from jax.experimental import pallas as pl
from jax.experimental.pallas import tpu as pltpu
from jax.sharding import PartitionSpec as P

NS_STEPS = 4
MIRROR = (1, 0, 3, 2, 5, 4)
MOVES = ((1, 0), (-1, 0), (0, 1), (0, -1))
REMOTE = len(MOVES)
MESH = pl.DeviceIdType.MESH
VMEM_LIMIT = 48 * 1024 * 1024


def dot32(left, right):
    return jnp.dot(left, right, preferred_element_type=jnp.float32)


def split(value):
    high = value.astype(jnp.bfloat16)
    return high, (value - high.astype(jnp.float32)).astype(jnp.bfloat16)


def inverses(matrices, exact):
    size = matrices[0].shape[0]
    row_id = lax.broadcasted_iota(jnp.int32, (size, size), 0)
    col_id = lax.broadcasted_iota(jnp.int32, (size, size), 1)
    identity = (row_id == col_id).astype(jnp.float32)
    lefts, iterates = [], []
    for matrix in matrices:
        magnitude = jnp.abs(matrix)
        column_norm = jnp.max(jnp.sum(magnitude, axis=0, keepdims=True), axis=1, keepdims=True)
        row_norm = jnp.max(jnp.sum(magnitude, axis=1, keepdims=True), axis=0, keepdims=True)
        iterates.append(matrix.T * (1.0 / (column_norm * row_norm)))
        high, low = split(matrix)
        lefts.append(jnp.concatenate([high, high] if exact else [high, high, low], axis=1))
    for _ in range(NS_STEPS):
        halves = [split(iterate) for iterate in iterates]
        rests = [
            identity - dot32(left, jnp.concatenate([high, low] if exact else [high, low, high], axis=0))
            for left, (high, low) in zip(lefts, halves)
        ]
        rests = [rest.astype(jnp.bfloat16) for rest in rests]
        iterates = [
            iterate + dot32(jnp.concatenate([high, low], axis=1), jnp.concatenate([rest, rest], axis=0))
            for iterate, (high, low), rest in zip(iterates, halves, rests)
        ]
    return [iterate.astype(jnp.bfloat16) for iterate in iterates]


def exchange(sizes, capacity, diag_ref, off_ref, inv_ref, got_off, got_inv, send_sem, recv_sem):
    here = (lax.axis_index("row"), lax.axis_index("col"))
    there, exists = [], []
    for move in MOVES:
        target = tuple(here[axis] + move[axis] for axis in range(2))
        axis = 0 if move[0] != 0 else 1
        there.append(target)
        exists.append((target[axis] < sizes[axis]) if move[axis] > 0 else (target[axis] >= 0))

    barrier = pltpu.get_barrier_semaphore()
    for side in range(REMOTE):
        @pl.when(exists[side])
        def _():
            pl.semaphore_signal(barrier, inc=1, device_id=there[side], device_id_type=MESH)
    pl.semaphore_wait(barrier, sum(flag.astype(jnp.int32) for flag in exists))

    def outgoing(kind, side):
        source, landing = ((off_ref.at[pl.ds(0, capacity), side], got_off), (inv_ref, got_inv))[kind]
        return pltpu.make_async_remote_copy(
            src_ref=source,
            dst_ref=landing.at[MIRROR[side]],
            send_sem=send_sem.at[kind, side],
            recv_sem=recv_sem.at[kind, MIRROR[side]],
            device_id=there[side],
            device_id_type=MESH,
        )

    def incoming(kind, side):
        landing = (got_off, got_inv)[kind]
        return pltpu.make_async_remote_copy(
            src_ref=landing.at[side],
            dst_ref=landing.at[side],
            send_sem=send_sem.at[kind, side],
            recv_sem=recv_sem.at[kind, side],
            device_id=there[side],
            device_id_type=MESH,
        )

    for side in (2, 3, 0, 1):
        @pl.when(exists[side])
        def _():
            outgoing(0, side).start()

    found = inverses([diag_ref[i].astype(jnp.float32) for i in range(capacity)], True)
    for i in range(capacity):
        inv_ref[i] = found[i]
    for side in (2, 3, 0, 1):
        @pl.when(exists[side])
        def _():
            outgoing(1, side).start()
    for side in range(REMOTE):
        @pl.when(exists[side])
        def _():
            for kind in range(2):
                outgoing(kind, side).wait_send()
                incoming(kind, side).wait_recv()


def finish(capacity, named_ref, level_ref, diag_ref, off_ref, inv_ref, got_off, got_inv, pivot_ref, factor_ref):
    rows, slots, size, _ = off_ref.shape
    start = rows - capacity
    zero = jnp.zeros((size, size), jnp.bfloat16)

    def scaled(i):
        wide = dot32(inv_ref[i], jnp.concatenate([off_ref[i, k] for k in range(slots)], axis=1))
        wide = wide.astype(jnp.bfloat16)
        return [
            jnp.where(named_ref[i, k] >= 0, wide[:, k * size : (k + 1) * size], zero)
            for k in range(slots)
        ]

    pivots = []
    for q in range(start, rows):
        lowers, facing = [], []
        for k in range(slots):
            named = named_ref[q, k]
            live = named >= 0
            local = jnp.minimum(lax.rem(jnp.maximum(named, 0), rows), capacity - 1)
            if k < REMOTE:
                across, faced = got_inv[k, local], got_off[k, local]
            else:
                across, faced = inv_ref[local], off_ref[local, MIRROR[k]]
            across = jnp.where(live, across, zero)
            mine = jnp.where(live, off_ref[q, k], zero)
            lowers.append(dot32(mine, across).astype(jnp.bfloat16))
            facing.append(jnp.where(live, faced, zero))
        schur = dot32(jnp.concatenate(lowers, axis=1), jnp.concatenate(facing, axis=0))
        pivots.append(diag_ref[q].astype(jnp.float32) - schur)
        if q < capacity:
            early = level_ref[q] == 0
            uppers = scaled(q)
            for k in range(slots):
                factor_ref[q, k] = jnp.where(early, uppers[k], lowers[k])
        else:
            for k in range(slots):
                factor_ref[q, k] = lowers[k]
    for i in range(start):
        uppers = scaled(i)
        for k in range(slots):
            factor_ref[i, k] = uppers[k]
        pivot_ref[i] = inv_ref[i]
    second = inverses(pivots, False)
    for q in range(start, rows):
        if q < capacity:
            pivot_ref[q] = jnp.where(level_ref[q] == 0, inv_ref[q], second[q - start])
        else:
            pivot_ref[q] = second[q - start]


def solution(mesh):
    sizes = (mesh.shape["row"], mesh.shape["col"])

    def shards(diag_blocks, off_blocks, neighbors, levels):
        rows, slots, size, _ = off_blocks.shape
        capacity = 3 * rows // 4
        dtype = jnp.bfloat16
        anywhere = pl.BlockSpec(memory_space=pl.ANY)
        vmem = pl.BlockSpec(memory_space=pltpu.VMEM)
        smem = pl.BlockSpec(memory_space=pltpu.SMEM)
        got = jax.ShapeDtypeStruct((REMOTE, capacity, size, size), dtype)
        inverse, got_off, got_inv = pl.pallas_call(
            lambda *refs: exchange(sizes, capacity, *refs),
            name="exchange",
            out_shape=(jax.ShapeDtypeStruct((capacity, size, size), dtype), got, got),
            in_specs=[vmem, anywhere],
            out_specs=(vmem, anywhere, anywhere),
            scratch_shapes=[
                pltpu.SemaphoreType.DMA((2, REMOTE)),
                pltpu.SemaphoreType.DMA((2, REMOTE)),
            ],
            compiler_params=pltpu.CompilerParams(
                collective_id=0, has_side_effects=True, vmem_limit_bytes=VMEM_LIMIT
            ),
        )(diag_blocks, off_blocks)
        return pl.pallas_call(
            lambda *refs: finish(capacity, *refs),
            name="finish",
            out_shape=(
                jax.ShapeDtypeStruct((rows, size, size), dtype),
                jax.ShapeDtypeStruct((rows, slots, size, size), dtype),
            ),
            in_specs=[smem, smem] + [vmem] * 5,
            out_specs=(vmem, vmem),
            compiler_params=pltpu.CompilerParams(vmem_limit_bytes=VMEM_LIMIT),
        )(neighbors, levels, diag_blocks, off_blocks, inverse, got_off, got_inv)

    blocks = P(("row", "col"), None, None)
    wide = P(("row", "col"), None, None, None)
    in_specs = (blocks, wide, P(("row", "col"), None), P(("row", "col")))
    return jax.shard_map(shards, mesh=mesh, in_specs=in_specs, out_specs=(blocks, wide), check_vma=False)
```

```python
import jax
import jax.numpy as jnp
from jax import lax
from jax.experimental import pallas as pl
from jax.experimental.pallas import tpu as pltpu
from jax.sharding import PartitionSpec as P

NS_STEPS = 4
MIRROR = (1, 0, 3, 2, 5, 4)
MOVES = ((1, 0), (-1, 0), (0, 1), (0, -1))
REMOTE = len(MOVES)
MESH = pl.DeviceIdType.MESH
VMEM_LIMIT = 40 * 1024 * 1024
SIDEWAYS = (0, 1)
ALONG = (2, 3)
INSIDE = (4, 5)


def dot32(left, right):
    return jnp.dot(left, right, preferred_element_type=jnp.float32)


def split(value):
    high = value.astype(jnp.bfloat16)
    return high, (value - high.astype(jnp.float32)).astype(jnp.bfloat16)


def inverses(matrices, exact):
    size = matrices[0].shape[0]
    row_id = lax.broadcasted_iota(jnp.int32, (size, size), 0)
    col_id = lax.broadcasted_iota(jnp.int32, (size, size), 1)
    identity = (row_id == col_id).astype(jnp.float32)
    lefts, iterates = [], []
    for matrix in matrices:
        magnitude = jnp.abs(matrix)
        column_norm = jnp.max(jnp.sum(magnitude, axis=0, keepdims=True), axis=1, keepdims=True)
        row_norm = jnp.max(jnp.sum(magnitude, axis=1, keepdims=True), axis=0, keepdims=True)
        iterates.append(matrix.T * (1.0 / (column_norm * row_norm)))
        high, low = split(matrix)
        lefts.append(jnp.concatenate([high, high] if exact else [high, high, low], axis=1))
    for _ in range(NS_STEPS):
        halves = [split(iterate) for iterate in iterates]
        rests = [
            identity - dot32(left, jnp.concatenate([high, low] if exact else [high, low, high], axis=0))
            for left, (high, low) in zip(lefts, halves)
        ]
        rests = [rest.astype(jnp.bfloat16) for rest in rests]
        iterates = [
            iterate + dot32(jnp.concatenate([high, low], axis=1), jnp.concatenate([rest, rest], axis=0))
            for iterate, (high, low), rest in zip(iterates, halves, rests)
        ]
    return [iterate.astype(jnp.bfloat16) for iterate in iterates]


def picker(named_ref, rows, capacity):
    def pick(q, k):
        named = named_ref[q, k]
        local = jnp.minimum(lax.rem(jnp.maximum(named, 0), rows), capacity - 1)
        return named >= 0, local

    return pick


def exchange(
    sizes, capacity, diag_hbm, off_hbm, named_hbm, level_hbm,
    inv_ref, part_ref, rest_ref, mine_ref, far_off, far_inv,
    diag_ref, off_ref, named_ref, level_ref, near_off, near_inv, local_sem, send_sem, recv_sem,
):
    rows, slots, size, _ = off_ref.shape
    start = rows - capacity
    zero = jnp.zeros((size, size), jnp.bfloat16)
    here = (lax.axis_index("row"), lax.axis_index("col"))
    there, exists = [], []
    for move in MOVES:
        target = tuple(here[axis] + move[axis] for axis in range(2))
        axis = 0 if move[0] != 0 else 1
        there.append(target)
        exists.append((target[axis] < sizes[axis]) if move[axis] > 0 else (target[axis] >= 0))

    barrier = pltpu.get_barrier_semaphore()
    for side in range(REMOTE):
        @pl.when(exists[side])
        def _():
            pl.semaphore_signal(barrier, inc=1, device_id=there[side], device_id_type=MESH)
    loads = [
        pltpu.make_async_copy(source, target, local_sem.at[i])
        for i, (source, target) in enumerate([
            (diag_hbm, diag_ref),
            (off_hbm, off_ref),
            (named_hbm, named_ref),
            (level_hbm, level_ref),
            (off_hbm.at[pl.ds(start, capacity), pl.ds(ALONG[0], 2)], mine_ref),
        ])
    ]
    for load in loads:
        load.start()
    pl.semaphore_wait(barrier, sum(flag.astype(jnp.int32) for flag in exists))

    def landing(kind, side):
        if side in ALONG:
            return (far_off, far_inv)[kind].at[side - ALONG[0]]
        return (near_off, near_inv)[kind].at[side]

    def transfer(kind, source, side, arrives):
        return pltpu.make_async_remote_copy(
            src_ref=source,
            dst_ref=landing(kind, arrives),
            send_sem=send_sem.at[kind, side],
            recv_sem=recv_sem.at[kind, arrives],
            device_id=there[side],
            device_id_type=MESH,
        )

    def outgoing(kind, side):
        source = inv_ref if kind else off_hbm.at[pl.ds(0, capacity), side]
        return transfer(kind, source, side, MIRROR[side])

    def incoming(kind, side):
        return transfer(kind, landing(kind, side), side, side)

    for side in ALONG + SIDEWAYS:
        @pl.when(exists[side])
        def _():
            outgoing(0, side).start()

    loads[0].wait()
    found = inverses([diag_ref[i].astype(jnp.float32) for i in range(capacity)], True)
    for i in range(capacity):
        inv_ref[i] = found[i]
    for side in ALONG + SIDEWAYS:
        @pl.when(exists[side])
        def _():
            outgoing(1, side).start()

    for load in loads[1:]:
        load.wait()
    pick = picker(named_ref, rows, capacity)
    for i in range(capacity):
        upper = dot32(inv_ref[i], jnp.concatenate([off_ref[i, k] for k in range(slots)], axis=1))
        upper = upper.astype(jnp.bfloat16)
        for k in range(slots):
            part_ref[i, k] = jnp.where(
                named_ref[i, k] >= 0, upper[:, k * size : (k + 1) * size], zero
            )

    def absorb(group, before):
        for q in range(start, rows):
            lowers, facing = [], []
            for k in group:
                live, local = pick(q, k)
                if k in INSIDE:
                    across, faced = inv_ref[local], off_ref[local, MIRROR[k]]
                else:
                    across, faced = near_inv[k, local], near_off[k, local]
                lower = dot32(
                    jnp.where(live, off_ref[q, k], zero), jnp.where(live, across, zero)
                ).astype(jnp.bfloat16)
                lowers.append(lower)
                facing.append(jnp.where(live, faced, zero))
                if q < capacity:
                    part_ref[q, k] = jnp.where(level_ref[q] == 0, part_ref[q, k], lower)
                else:
                    part_ref[q, k] = lower
            schur = dot32(jnp.concatenate(lowers, axis=1), jnp.concatenate(facing, axis=0))
            rest_ref[q - start] = before(q) - schur

    absorb(INSIDE, lambda q: diag_ref[q].astype(jnp.float32))
    for side in SIDEWAYS:
        @pl.when(exists[side])
        def _():
            for kind in range(2):
                incoming(kind, side).wait_recv()
    absorb(SIDEWAYS, lambda q: rest_ref[q - start])
    for side in ALONG:
        @pl.when(exists[side])
        def _():
            for kind in range(2):
                incoming(kind, side).wait_recv()
    for side in range(REMOTE):
        @pl.when(exists[side])
        def _():
            for kind in range(2):
                outgoing(kind, side).wait_send()


def finish(
    capacity, named_ref, level_ref, inv_ref, part_ref, rest_ref, mine_ref, far_off, far_inv,
    pivot_hbm, factor_hbm, pivot_ref, lower_ref, sems,
):
    rows, slots, size, _ = part_ref.shape
    start = rows - capacity
    zero = jnp.zeros((size, size), jnp.bfloat16)
    late = pl.ds(start, capacity)
    soon = pl.ds(0, start)
    stores = [
        pltpu.make_async_copy(source, target, sems.at[i])
        for i, (source, target) in enumerate([
            (part_ref.at[soon], factor_hbm.at[soon]),
            (part_ref.at[late, pl.ds(SIDEWAYS[0], 2)], factor_hbm.at[late, pl.ds(SIDEWAYS[0], 2)]),
            (part_ref.at[late, pl.ds(INSIDE[0], 2)], factor_hbm.at[late, pl.ds(INSIDE[0], 2)]),
            (inv_ref.at[soon], pivot_hbm.at[soon]),
            (lower_ref, factor_hbm.at[late, pl.ds(ALONG[0], 2)]),
            (pivot_ref, pivot_hbm.at[late]),
        ])
    ]
    for store in stores[:4]:
        store.start()
    pick = picker(named_ref, rows, capacity)
    pivots = []
    for q in range(start, rows):
        lowers, facing = [], []
        for j, k in enumerate(ALONG):
            live, local = pick(q, k)
            lower = dot32(
                jnp.where(live, mine_ref[q - start, j], zero), jnp.where(live, far_inv[j, local], zero)
            ).astype(jnp.bfloat16)
            lowers.append(lower)
            facing.append(jnp.where(live, far_off[j, local], zero))
            if q < capacity:
                lower = jnp.where(level_ref[q] == 0, part_ref[q, k], lower)
            lower_ref[q - start, j] = lower
        schur = dot32(jnp.concatenate(lowers, axis=1), jnp.concatenate(facing, axis=0))
        pivots.append(rest_ref[q - start] - schur)
    stores[4].start()
    second = inverses(pivots, False)
    for q in range(start, rows):
        value = second[q - start]
        if q < capacity:
            value = jnp.where(level_ref[q] == 0, inv_ref[q], value)
        pivot_ref[q - start] = value
    stores[5].start()
    for store in stores:
        store.wait()


def solution(mesh):
    sizes = (mesh.shape["row"], mesh.shape["col"])

    def shards(diag_blocks, off_blocks, neighbors, levels):
        rows, slots, size, _ = off_blocks.shape
        capacity = 3 * rows // 4
        block = (size, size)
        hbm = pl.BlockSpec(memory_space=pltpu.HBM)
        vmem = pl.BlockSpec(memory_space=pltpu.VMEM)
        smem = pl.BlockSpec(memory_space=pltpu.SMEM)

        def shape(*lead, dtype=jnp.bfloat16):
            return jax.ShapeDtypeStruct(lead + block, dtype)

        def room(*lead):
            return pltpu.VMEM(lead + block, jnp.bfloat16)

        carried = pl.pallas_call(
            lambda *refs: exchange(sizes, capacity, *refs),
            name="exchange",
            out_shape=(
                shape(capacity),
                shape(rows, slots),
                shape(capacity, dtype=jnp.float32),
                shape(capacity, 2),
                shape(2, capacity),
                shape(2, capacity),
            ),
            in_specs=[hbm] * 4,
            out_specs=(vmem,) * 6,
            scratch_shapes=[
                room(rows),
                room(rows, slots),
                pltpu.SMEM(neighbors.shape, jnp.int32),
                pltpu.SMEM(levels.shape, jnp.int32),
                room(2, capacity),
                room(2, capacity),
                pltpu.SemaphoreType.DMA((5,)),
                pltpu.SemaphoreType.DMA((2, REMOTE)),
                pltpu.SemaphoreType.DMA((2, REMOTE)),
            ],
            compiler_params=pltpu.CompilerParams(
                collective_id=0, has_side_effects=True, vmem_limit_bytes=VMEM_LIMIT
            ),
        )(*[pltpu.with_memory_space_constraint(x, pltpu.HBM) for x in (diag_blocks, off_blocks, neighbors, levels)])
        return pl.pallas_call(
            lambda *refs: finish(capacity, *refs),
            name="finish",
            out_shape=(shape(rows), shape(rows, slots)),
            in_specs=[smem] * 2 + [vmem] * 6,
            out_specs=(hbm, hbm),
            scratch_shapes=[room(capacity), room(capacity, 2), pltpu.SemaphoreType.DMA((6,))],
            compiler_params=pltpu.CompilerParams(vmem_limit_bytes=VMEM_LIMIT),
        )(neighbors, levels, *carried)

    blocks = P(("row", "col"), None, None)
    wide = P(("row", "col"), None, None, None)
    in_specs = (blocks, wide, P(("row", "col"), None), P(("row", "col")))
    return jax.shard_map(shards, mesh=mesh, in_specs=in_specs, out_specs=(blocks, wide), check_vma=False)
```

```python
import jax
import jax.numpy as jnp
from jax import lax
from jax.experimental import pallas as pl
from jax.experimental.pallas import tpu as pltpu
from jax.sharding import PartitionSpec as P

NS_STEPS = 4
MIRROR = (1, 0, 3, 2, 5, 4)
MOVES = ((1, 0), (-1, 0), (0, 1), (0, -1))
REMOTE = len(MOVES)
MESH = pl.DeviceIdType.MESH
VMEM_LIMIT = 40 * 1024 * 1024
SIDEWAYS = (0, 1)
ALONG = (2, 3)
INSIDE = (4, 5)


def dot32(left, right):
    return jnp.dot(left, right, preferred_element_type=jnp.float32)


def split(value):
    high = value.astype(jnp.bfloat16)
    return high, (value - high.astype(jnp.float32)).astype(jnp.bfloat16)


def inverses(matrices, paired):
    size = matrices[0].shape[0]
    row_id = lax.broadcasted_iota(jnp.int32, (size, size), 0)
    col_id = lax.broadcasted_iota(jnp.int32, (size, size), 1)
    identity = (row_id == col_id).astype(jnp.float32)
    iterates = []
    for matrix in matrices:
        magnitude = jnp.abs(matrix)
        column_norm = jnp.max(jnp.sum(magnitude, axis=0, keepdims=True), axis=1, keepdims=True)
        row_norm = jnp.max(jnp.sum(magnitude, axis=1, keepdims=True), axis=0, keepdims=True)
        iterates.append(matrix.T * (1.0 / (column_norm * row_norm)))
    lefts = [matrix.astype(jnp.bfloat16) for matrix in matrices]
    if paired:
        lefts = [jnp.concatenate([left, left], axis=1) for left in lefts]
    for _ in range(NS_STEPS):
        halves = [split(iterate) if paired else (iterate.astype(jnp.bfloat16),) for iterate in iterates]
        rests = [
            (identity - dot32(left, jnp.concatenate(half, axis=0))).astype(jnp.bfloat16)
            for left, half in zip(lefts, halves)
        ]
        iterates = [
            iterate + dot32(jnp.concatenate(half, axis=1), jnp.concatenate([rest] * len(half), axis=0))
            for iterate, half, rest in zip(iterates, halves, rests)
        ]
    return [iterate.astype(jnp.bfloat16) for iterate in iterates]


def picker(named_ref, rows, capacity):
    def pick(q, k):
        named = named_ref[q, k]
        local = jnp.minimum(lax.rem(jnp.maximum(named, 0), rows), capacity - 1)
        return named >= 0, local

    return pick


def exchange(
    sizes, capacity, diag_hbm, off_hbm, named_hbm, level_hbm,
    inv_ref, part_ref, rest_ref, lower_ref, far_off,
    far_inv, diag_ref, off_ref, named_ref, level_ref, near_off, near_inv, local_sem, send_sem, recv_sem,
):
    rows, slots, size, _ = off_ref.shape
    start = rows - capacity
    zero = jnp.zeros((size, size), jnp.bfloat16)
    here = (lax.axis_index("row"), lax.axis_index("col"))
    there, exists = [], []
    for move in MOVES:
        target = tuple(here[axis] + move[axis] for axis in range(2))
        axis = 0 if move[0] != 0 else 1
        there.append(target)
        exists.append((target[axis] < sizes[axis]) if move[axis] > 0 else (target[axis] >= 0))

    barrier = pltpu.get_barrier_semaphore()
    for side in range(REMOTE):
        @pl.when(exists[side])
        def _():
            pl.semaphore_signal(barrier, inc=1, device_id=there[side], device_id_type=MESH)
    loads = [
        pltpu.make_async_copy(source, target, local_sem.at[i])
        for i, (source, target) in enumerate([
            (diag_hbm, diag_ref),
            (off_hbm, off_ref),
            (named_hbm, named_ref),
            (level_hbm, level_ref),
        ])
    ]
    for load in loads:
        load.start()
    pl.semaphore_wait(barrier, sum(flag.astype(jnp.int32) for flag in exists))

    pieces = (pl.ds(0, capacity - 1), pl.ds(0, capacity), pl.ds(capacity - 1, 1))

    def piece(kind, side):
        return pieces[1] if side in SIDEWAYS else pieces[kind]

    def landing(kind, side):
        if side in ALONG:
            target = (far_off, far_inv, far_off)[kind].at[side - ALONG[0]]
        else:
            target = (near_off, near_inv)[kind].at[side]
        return target.at[piece(kind, side)]

    def transfer(kind, source, side, arrives):
        return pltpu.make_async_remote_copy(
            src_ref=source,
            dst_ref=landing(kind, arrives),
            send_sem=send_sem.at[kind, side],
            recv_sem=recv_sem.at[kind, arrives],
            device_id=there[side],
            device_id_type=MESH,
        )

    def outgoing(kind, side):
        source = inv_ref if kind == 1 else off_hbm.at[piece(kind, side), side]
        return transfer(kind, source, side, MIRROR[side])

    def incoming(kind, side):
        return transfer(kind, landing(kind, side), side, side)

    for side in ALONG + SIDEWAYS:
        @pl.when(exists[side])
        def _():
            outgoing(0, side).start()

    loads[0].wait()
    found = inverses([diag_ref[i].astype(jnp.float32) for i in range(capacity)], True)
    for i in range(capacity):
        inv_ref[i] = found[i]
    for side in ALONG + SIDEWAYS:
        @pl.when(exists[side])
        def _():
            outgoing(1, side).start()
            if side in ALONG:
                outgoing(2, side).start()

    for load in loads[1:]:
        load.wait()
    pick = picker(named_ref, rows, capacity)
    for i in range(capacity):
        upper = dot32(inv_ref[i], jnp.concatenate([off_ref[i, k] for k in range(slots)], axis=1))
        upper = upper.astype(jnp.bfloat16)
        for k in range(slots):
            part_ref[i, k] = jnp.where(
                named_ref[i, k] >= 0, upper[:, k * size : (k + 1) * size], zero
            )

    def lower_blocks(q, group):
        lowers = []
        for k in group:
            live, local = pick(q, k)
            if k in INSIDE:
                across = inv_ref[local]
            elif k in SIDEWAYS:
                across = near_inv[k, local]
            else:
                across = far_inv[k - ALONG[0], local]
            lower = dot32(off_ref[q, k], jnp.where(live, across, zero)).astype(jnp.bfloat16)
            lowers.append(lower)
            if q < capacity:
                lower = jnp.where(level_ref[q] == 0, part_ref[q, k], lower)
            part_ref[q, k] = lower
        return lowers

    def absorb(group, before):
        for q in range(start, rows):
            facing = []
            for k in group:
                live, local = pick(q, k)
                faced = off_ref[local, MIRROR[k]] if k in INSIDE else near_off[k, local]
                facing.append(jnp.where(live, faced, zero))
            lowers = lower_blocks(q, group)
            schur = dot32(jnp.concatenate(lowers, axis=1), jnp.concatenate(facing, axis=0))
            rest_ref[q - start] = before(q) - schur

    absorb(INSIDE, lambda q: diag_ref[q].astype(jnp.float32))
    for side in SIDEWAYS:
        @pl.when(exists[side])
        def _():
            for kind in range(2):
                incoming(kind, side).wait_recv()
    absorb(SIDEWAYS, lambda q: rest_ref[q - start])
    for side in ALONG:
        @pl.when(exists[side])
        def _():
            incoming(1, side).wait_recv()
    for q in range(start, rows):
        for j, lower in enumerate(lower_blocks(q, ALONG)):
            lower_ref[q - start, j] = lower
    for side in ALONG:
        @pl.when(exists[side])
        def _():
            incoming(0, side).wait_recv()
            incoming(2, side).wait_recv()
    for side in range(REMOTE):
        @pl.when(exists[side])
        def _():
            for kind in range(3 if side in ALONG else 2):
                outgoing(kind, side).wait_send()


def finish(
    capacity, named_ref, level_ref, inv_ref, part_ref, rest_ref, lower_ref, far_off, pivot_hbm, factor_hbm, pivot_ref, sems
):
    rows, slots, size, _ = part_ref.shape
    start = rows - capacity
    zero = jnp.zeros((size, size), jnp.bfloat16)
    soon = pl.ds(0, start)
    stores = [
        pltpu.make_async_copy(source, target, sems.at[i])
        for i, (source, target) in enumerate([
            (part_ref, factor_hbm),
            (inv_ref.at[soon], pivot_hbm.at[soon]),
            (pivot_ref, pivot_hbm.at[pl.ds(start, capacity)]),
        ])
    ]
    stores[0].start()
    stores[1].start()
    pick = picker(named_ref, rows, capacity)
    pivots = []
    for q in range(start, rows):
        facing = []
        for j, k in enumerate(ALONG):
            live, local = pick(q, k)
            facing.append(jnp.where(live, far_off[j, local], zero))
        lowers = [lower_ref[q - start, j] for j in range(len(ALONG))]
        schur = dot32(jnp.concatenate(lowers, axis=1), jnp.concatenate(facing, axis=0))
        pivots.append(rest_ref[q - start] - schur)
    second = inverses(pivots, False)
    for q in range(start, rows):
        value = second[q - start]
        if q < capacity:
            value = jnp.where(level_ref[q] == 0, inv_ref[q], value)
        pivot_ref[q - start] = value
    stores[2].start()
    for store in stores:
        store.wait()


def solution(mesh):
    sizes = (mesh.shape["row"], mesh.shape["col"])

    def shards(diag_blocks, off_blocks, neighbors, levels):
        rows, slots, size, _ = off_blocks.shape
        capacity = 3 * rows // 4
        block = (size, size)
        hbm = pl.BlockSpec(memory_space=pltpu.HBM)
        vmem = pl.BlockSpec(memory_space=pltpu.VMEM)
        smem = pl.BlockSpec(memory_space=pltpu.SMEM)

        def shape(*lead, dtype=jnp.bfloat16):
            return jax.ShapeDtypeStruct(lead + block, dtype)

        def room(*lead):
            return pltpu.VMEM(lead + block, jnp.bfloat16)

        carried = pl.pallas_call(
            lambda *refs: exchange(sizes, capacity, *refs),
            name="exchange",
            out_shape=(
                shape(capacity),
                shape(rows, slots),
                shape(capacity, dtype=jnp.float32),
                shape(capacity, 2),
                shape(2, capacity),
            ),
            in_specs=[hbm] * 4,
            out_specs=(vmem,) * 5,
            scratch_shapes=[
                room(2, capacity),
                room(rows),
                room(rows, slots),
                pltpu.SMEM(neighbors.shape, jnp.int32),
                pltpu.SMEM(levels.shape, jnp.int32),
                room(2, capacity),
                room(2, capacity),
                pltpu.SemaphoreType.DMA((4,)),
                pltpu.SemaphoreType.DMA((3, REMOTE)),
                pltpu.SemaphoreType.DMA((3, REMOTE)),
            ],
            compiler_params=pltpu.CompilerParams(
                collective_id=0, has_side_effects=True, vmem_limit_bytes=VMEM_LIMIT
            ),
        )(*[pltpu.with_memory_space_constraint(x, pltpu.HBM) for x in (diag_blocks, off_blocks, neighbors, levels)])
        return pl.pallas_call(
            lambda *refs: finish(capacity, *refs),
            name="finish",
            out_shape=(shape(rows), shape(rows, slots)),
            in_specs=[smem] * 2 + [vmem] * 5,
            out_specs=(hbm, hbm),
            scratch_shapes=[room(capacity), pltpu.SemaphoreType.DMA((3,))],
            compiler_params=pltpu.CompilerParams(vmem_limit_bytes=VMEM_LIMIT),
        )(neighbors, levels, *carried)

    blocks = P(("row", "col"), None, None)
    wide = P(("row", "col"), None, None, None)
    in_specs = (blocks, wide, P(("row", "col"), None), P(("row", "col")))
    return jax.shard_map(shards, mesh=mesh, in_specs=in_specs, out_specs=(blocks, wide), check_vma=False)
```

```python
import jax
import jax.numpy as jnp
from jax import lax
from jax.experimental import pallas as pl
from jax.experimental.pallas import tpu as pltpu
from jax.sharding import PartitionSpec as P

NS_STEPS = 4
MIRROR = (1, 0, 3, 2, 5, 4)
MOVES = ((1, 0), (-1, 0), (0, 1), (0, -1))
REMOTE = len(MOVES)
MESH = pl.DeviceIdType.MESH
VMEM_LIMIT = 40 * 1024 * 1024
SIDEWAYS = (0, 1)
ALONG = (2, 3)
INSIDE = (4, 5)


def dot32(left, right):
    return jnp.dot(left, right, preferred_element_type=jnp.float32)


def split(value):
    high = value.astype(jnp.bfloat16)
    return high, (value - high.astype(jnp.float32)).astype(jnp.bfloat16)


def inverses(matrices, paired):
    size = matrices[0].shape[0]
    row_id = lax.broadcasted_iota(jnp.int32, (size, size), 0)
    col_id = lax.broadcasted_iota(jnp.int32, (size, size), 1)
    identity = (row_id == col_id).astype(jnp.float32)
    iterates = []
    for matrix in matrices:
        magnitude = jnp.abs(matrix)
        column_norm = jnp.max(jnp.sum(magnitude, axis=0, keepdims=True), axis=1, keepdims=True)
        row_norm = jnp.max(jnp.sum(magnitude, axis=1, keepdims=True), axis=0, keepdims=True)
        iterates.append(matrix.T * (1.0 / (column_norm * row_norm)))
    lefts = [matrix.astype(jnp.bfloat16) for matrix in matrices]
    if paired:
        lefts = [jnp.concatenate([left, left], axis=1) for left in lefts]
    for _ in range(NS_STEPS):
        halves = [split(iterate) if paired else (iterate.astype(jnp.bfloat16),) for iterate in iterates]
        rests = [
            (identity - dot32(left, jnp.concatenate(half, axis=0))).astype(jnp.bfloat16)
            for left, half in zip(lefts, halves)
        ]
        iterates = [
            iterate + dot32(jnp.concatenate(half, axis=1), jnp.concatenate([rest] * len(half), axis=0))
            for iterate, half, rest in zip(iterates, halves, rests)
        ]
    return [iterate.astype(jnp.bfloat16) for iterate in iterates]


def picker(named_ref, rows, capacity):
    def pick(q, k):
        named = named_ref[q, k]
        local = jnp.minimum(lax.rem(jnp.maximum(named, 0), rows), capacity - 1)
        return named >= 0, local

    return pick


def exchange(
    sizes, capacity, diag_hbm, off_hbm, named_hbm, level_hbm,
    pivot_ref, part_ref,
    inv_ref, rest_ref, lower_ref, far_off, far_inv, diag_ref, off_ref, named_ref, level_ref, near_off, near_inv, local_sem, send_sem, recv_sem,
):
    rows, slots, size, _ = off_ref.shape
    start = rows - capacity
    zero = jnp.zeros((size, size), jnp.bfloat16)
    here = (lax.axis_index("row"), lax.axis_index("col"))
    there, exists = [], []
    for move in MOVES:
        target = tuple(here[axis] + move[axis] for axis in range(2))
        axis = 0 if move[0] != 0 else 1
        there.append(target)
        exists.append((target[axis] < sizes[axis]) if move[axis] > 0 else (target[axis] >= 0))

    barrier = pltpu.get_barrier_semaphore()
    for side in range(REMOTE):
        @pl.when(exists[side])
        def _():
            pl.semaphore_signal(barrier, inc=1, device_id=there[side], device_id_type=MESH)
    loads = [
        pltpu.make_async_copy(source, target, local_sem.at[i])
        for i, (source, target) in enumerate([
            (diag_hbm, diag_ref),
            (off_hbm, off_ref),
            (named_hbm, named_ref),
            (level_hbm, level_ref),
        ])
    ]
    for load in loads:
        load.start()
    pl.semaphore_wait(barrier, sum(flag.astype(jnp.int32) for flag in exists))

    pieces = (pl.ds(0, capacity - 1), pl.ds(0, capacity), pl.ds(capacity - 1, 1))

    def piece(kind, side):
        return pieces[1] if side in SIDEWAYS else pieces[kind]

    def landing(kind, side):
        if side in ALONG:
            target = (far_off, far_inv, far_off)[kind].at[side - ALONG[0]]
        else:
            target = (near_off, near_inv)[kind].at[side]
        return target.at[piece(kind, side)]

    def transfer(kind, source, side, arrives):
        return pltpu.make_async_remote_copy(
            src_ref=source,
            dst_ref=landing(kind, arrives),
            send_sem=send_sem.at[kind, side],
            recv_sem=recv_sem.at[kind, arrives],
            device_id=there[side],
            device_id_type=MESH,
        )

    def outgoing(kind, side):
        source = inv_ref if kind == 1 else off_hbm.at[piece(kind, side), side]
        return transfer(kind, source, side, MIRROR[side])

    def incoming(kind, side):
        return transfer(kind, landing(kind, side), side, side)

    for side in ALONG + SIDEWAYS:
        @pl.when(exists[side])
        def _():
            outgoing(0, side).start()

    loads[0].wait()
    found = inverses([diag_ref[i].astype(jnp.float32) for i in range(capacity)], True)
    for i in range(capacity):
        inv_ref[i] = found[i]
    for side in ALONG + SIDEWAYS:
        @pl.when(exists[side])
        def _():
            outgoing(1, side).start()
            if side in ALONG:
                outgoing(2, side).start()

    for load in loads[1:]:
        load.wait()
    pick = picker(named_ref, rows, capacity)
    for i in range(capacity):
        upper = dot32(inv_ref[i], jnp.concatenate([off_ref[i, k] for k in range(slots)], axis=1))
        upper = upper.astype(jnp.bfloat16)
        for k in range(slots):
            part_ref[i, k] = jnp.where(
                named_ref[i, k] >= 0, upper[:, k * size : (k + 1) * size], zero
            )

    def lower_blocks(q, group):
        lowers = []
        for k in group:
            live, local = pick(q, k)
            if k in INSIDE:
                across = inv_ref[local]
            elif k in SIDEWAYS:
                across = near_inv[k, local]
            else:
                across = far_inv[k - ALONG[0], local]
            lower = dot32(off_ref[q, k], jnp.where(live, across, zero)).astype(jnp.bfloat16)
            lowers.append(lower)
            if q < capacity:
                lower = jnp.where(level_ref[q] == 0, part_ref[q, k], lower)
            part_ref[q, k] = lower
        return lowers

    def absorb(group, before):
        for q in range(start, rows):
            facing = []
            for k in group:
                live, local = pick(q, k)
                faced = off_ref[local, MIRROR[k]] if k in INSIDE else near_off[k, local]
                facing.append(jnp.where(live, faced, zero))
            lowers = lower_blocks(q, group)
            schur = dot32(jnp.concatenate(lowers, axis=1), jnp.concatenate(facing, axis=0))
            rest_ref[q - start] = before(q) - schur

    absorb(INSIDE, lambda q: diag_ref[q].astype(jnp.float32))
    for side in SIDEWAYS:
        @pl.when(exists[side])
        def _():
            for kind in range(2):
                incoming(kind, side).wait_recv()
    absorb(SIDEWAYS, lambda q: rest_ref[q - start])
    for side in ALONG:
        @pl.when(exists[side])
        def _():
            incoming(1, side).wait_recv()
    for q in range(start, rows):
        for j, lower in enumerate(lower_blocks(q, ALONG)):
            lower_ref[q - start, j] = lower
    for side in ALONG:
        @pl.when(exists[side])
        def _():
            incoming(0, side).wait_recv()
            incoming(2, side).wait_recv()
    pivots = []
    for q in range(start, rows):
        facing = []
        for j, k in enumerate(ALONG):
            live, local = pick(q, k)
            facing.append(jnp.where(live, far_off[j, local], zero))
        lowers = [lower_ref[q - start, j] for j in range(len(ALONG))]
        schur = dot32(jnp.concatenate(lowers, axis=1), jnp.concatenate(facing, axis=0))
        pivots.append(rest_ref[q - start] - schur)
    second = inverses(pivots, False)
    for i in range(rows):
        if i < start:
            value = inv_ref[i]
        elif i < capacity:
            value = jnp.where(level_ref[i] == 0, inv_ref[i], second[i - start])
        else:
            value = second[i - start]
        pivot_ref[i] = value
    for side in range(REMOTE):
        @pl.when(exists[side])
        def _():
            for kind in range(3 if side in ALONG else 2):
                outgoing(kind, side).wait_send()


def store(pivot_ref, part_ref, pivot_hbm, factor_hbm, sems):
    rows = part_ref.shape[0]
    copies = [
        pltpu.make_async_copy(part_ref.at[i], factor_hbm.at[i], sems.at[i]) for i in range(rows)
    ] + [pltpu.make_async_copy(pivot_ref, pivot_hbm, sems.at[rows])]
    for copy in copies:
        copy.start()
    for copy in copies:
        copy.wait()


def solution(mesh):
    sizes = (mesh.shape["row"], mesh.shape["col"])

    def shards(diag_blocks, off_blocks, neighbors, levels):
        rows, slots, size, _ = off_blocks.shape
        capacity = 3 * rows // 4
        block = (size, size)
        hbm = pl.BlockSpec(memory_space=pltpu.HBM)
        vmem = pl.BlockSpec(memory_space=pltpu.VMEM)

        def shape(*lead):
            return jax.ShapeDtypeStruct(lead + block, jnp.bfloat16)

        def room(*lead):
            return pltpu.VMEM(lead + block, jnp.bfloat16)

        carried = pl.pallas_call(
            lambda *refs: exchange(sizes, capacity, *refs),
            name="exchange",
            out_shape=(shape(rows), shape(rows, slots)),
            in_specs=[hbm] * 4,
            out_specs=(vmem, vmem),
            scratch_shapes=[
                room(capacity),
                pltpu.VMEM((capacity,) + block, jnp.float32),
                room(capacity, 2),
                room(2, capacity),
                room(2, capacity),
                room(rows),
                room(rows, slots),
                pltpu.SMEM(neighbors.shape, jnp.int32),
                pltpu.SMEM(levels.shape, jnp.int32),
                room(2, capacity),
                room(2, capacity),
                pltpu.SemaphoreType.DMA((4,)),
                pltpu.SemaphoreType.DMA((3, REMOTE)),
                pltpu.SemaphoreType.DMA((3, REMOTE)),
            ],
            compiler_params=pltpu.CompilerParams(
                collective_id=0, has_side_effects=True, vmem_limit_bytes=VMEM_LIMIT
            ),
        )(*[pltpu.with_memory_space_constraint(x, pltpu.HBM) for x in (diag_blocks, off_blocks, neighbors, levels)])
        return pl.pallas_call(
            store,
            name="store",
            out_shape=(shape(rows), shape(rows, slots)),
            in_specs=[vmem] * 2,
            out_specs=(hbm, hbm),
            scratch_shapes=[pltpu.SemaphoreType.DMA((rows + 1,))],
            compiler_params=pltpu.CompilerParams(vmem_limit_bytes=VMEM_LIMIT),
        )(*carried)

    blocks = P(("row", "col"), None, None)
    wide = P(("row", "col"), None, None, None)
    in_specs = (blocks, wide, P(("row", "col"), None), P(("row", "col")))
    return jax.shard_map(shards, mesh=mesh, in_specs=in_specs, out_specs=(blocks, wide), check_vma=False)
```

```python
import jax
import jax.numpy as jnp
from jax import lax
from jax.experimental import pallas as pl
from jax.experimental.pallas import tpu as pltpu
from jax.sharding import PartitionSpec as P

NS_STEPS = 4
MIRROR = (1, 0, 3, 2, 5, 4)
MOVES = ((1, 0), (-1, 0), (0, 1), (0, -1))
REMOTE = len(MOVES)
MESH = pl.DeviceIdType.MESH
VMEM_LIMIT = 40 * 1024 * 1024
SIDEWAYS = (0, 1)
ALONG = (2, 3)
INSIDE = (4, 5)


def dot32(left, right):
    return jnp.dot(left, right, preferred_element_type=jnp.float32)


def split(value):
    high = value.astype(jnp.bfloat16)
    return high, (value - high.astype(jnp.float32)).astype(jnp.bfloat16)


def inverses(matrices, paired):
    size = matrices[0].shape[0]
    row_id = lax.broadcasted_iota(jnp.int32, (size, size), 0)
    col_id = lax.broadcasted_iota(jnp.int32, (size, size), 1)
    identity = (row_id == col_id).astype(jnp.float32)
    iterates = []
    for matrix in matrices:
        magnitude = jnp.abs(matrix)
        column_norm = jnp.max(jnp.sum(magnitude, axis=0, keepdims=True), axis=1, keepdims=True)
        row_norm = jnp.max(jnp.sum(magnitude, axis=1, keepdims=True), axis=0, keepdims=True)
        iterates.append(matrix.T * (1.0 / (column_norm * row_norm)))
    lefts = [matrix.astype(jnp.bfloat16) for matrix in matrices]
    if paired:
        lefts = [jnp.concatenate([left, left], axis=1) for left in lefts]
    for _ in range(NS_STEPS):
        halves = [split(iterate) if paired else (iterate.astype(jnp.bfloat16),) for iterate in iterates]
        rests = [
            (identity - dot32(left, jnp.concatenate(half, axis=0))).astype(jnp.bfloat16)
            for left, half in zip(lefts, halves)
        ]
        iterates = [
            iterate + dot32(jnp.concatenate(half, axis=1), jnp.concatenate([rest] * len(half), axis=0))
            for iterate, half, rest in zip(iterates, halves, rests)
        ]
    return [iterate.astype(jnp.bfloat16) for iterate in iterates]


def picker(named_ref, rows, capacity):
    def pick(q, k):
        named = named_ref[q, k]
        local = jnp.minimum(lax.rem(jnp.maximum(named, 0), rows), capacity - 1)
        return named >= 0, local

    return pick


def exchange(
    sizes, capacity, diag_hbm, off_hbm, named_hbm, level_hbm,
    pivot_ref, part_ref,
    inv_ref, rest_ref, lower_ref, far_off, far_inv, diag_ref, off_ref, named_ref, level_ref, near_off, near_inv, local_sem, send_sem, recv_sem, answer,
):
    rows, slots, size, _ = off_ref.shape
    start = rows - capacity
    zero = jnp.zeros((size, size), jnp.bfloat16)
    here = (lax.axis_index("row"), lax.axis_index("col"))
    there, exists = [], []
    for move in MOVES:
        target = tuple(here[axis] + move[axis] for axis in range(2))
        axis = 0 if move[0] != 0 else 1
        there.append(target)
        exists.append((target[axis] < sizes[axis]) if move[axis] > 0 else (target[axis] >= 0))

    barrier = pltpu.get_barrier_semaphore()
    odd = lax.rem(here[0], 2) == 1
    even = jnp.logical_not(odd)
    for side in range(REMOTE):
        @pl.when(exists[side] if side in ALONG else jnp.logical_and(exists[side], odd))
        def _():
            pl.semaphore_signal(barrier, inc=1, device_id=there[side], device_id_type=MESH)
    loads = [
        pltpu.make_async_copy(source, target, local_sem.at[i])
        for i, (source, target) in enumerate([
            (diag_hbm, diag_ref),
            (off_hbm, off_ref),
            (named_hbm, named_ref),
            (level_hbm, level_ref),
        ])
    ]
    for load in loads:
        load.start()
    pl.semaphore_wait(barrier, sum(
        (exists[side] if side in ALONG else jnp.logical_and(exists[side], even)).astype(jnp.int32)
        for side in range(REMOTE)
    ))

    pieces = (pl.ds(0, capacity - 1), pl.ds(0, capacity), pl.ds(capacity - 1, 1))

    def piece(kind, side):
        return pieces[1] if side in SIDEWAYS else pieces[kind]

    def landing(kind, side):
        if side in ALONG:
            target = (far_off, far_inv, far_off)[kind].at[side - ALONG[0]]
        else:
            target = (near_off, near_inv)[kind].at[side]
        return target.at[piece(kind, side)]

    def transfer(kind, source, side, arrives):
        return pltpu.make_async_remote_copy(
            src_ref=source,
            dst_ref=landing(kind, arrives),
            send_sem=send_sem.at[kind, side],
            recv_sem=recv_sem.at[kind, arrives],
            device_id=there[side],
            device_id_type=MESH,
        )

    def outgoing(kind, side):
        source = inv_ref if kind == 1 else off_hbm.at[piece(kind, side), side]
        return transfer(kind, source, side, MIRROR[side])

    def incoming(kind, side):
        return transfer(kind, landing(kind, side), side, side)

    for side in ALONG:
        @pl.when(exists[side])
        def _():
            outgoing(0, side).start()
    for side in SIDEWAYS:
        @pl.when(jnp.logical_and(exists[side], even))
        def _():
            pl.semaphore_signal(
                answer.at[MIRROR[side]], inc=1, device_id=there[side], device_id_type=MESH
            )
            outgoing(0, side).start()

    loads[0].wait()
    found = inverses([diag_ref[i].astype(jnp.float32) for i in range(capacity)], True)
    for i in range(capacity):
        inv_ref[i] = found[i]
    for side in ALONG:
        @pl.when(exists[side])
        def _():
            outgoing(1, side).start()
            outgoing(2, side).start()
    for side in SIDEWAYS:
        @pl.when(jnp.logical_and(exists[side], even))
        def _():
            outgoing(1, side).start()

        @pl.when(jnp.logical_and(exists[side], odd))
        def _():
            pl.semaphore_wait(answer.at[side], 1)
            outgoing(0, side).start()
            outgoing(1, side).start()

    for load in loads[1:]:
        load.wait()
    pick = picker(named_ref, rows, capacity)
    for i in range(capacity):
        upper = dot32(inv_ref[i], jnp.concatenate([off_ref[i, k] for k in range(slots)], axis=1))
        upper = upper.astype(jnp.bfloat16)
        for k in range(slots):
            part_ref[i, k] = jnp.where(
                named_ref[i, k] >= 0, upper[:, k * size : (k + 1) * size], zero
            )

    def lower_blocks(q, group):
        lowers = []
        for k in group:
            live, local = pick(q, k)
            if k in INSIDE:
                across = inv_ref[local]
            elif k in SIDEWAYS:
                across = near_inv[k, local]
            else:
                across = far_inv[k - ALONG[0], local]
            lower = dot32(off_ref[q, k], jnp.where(live, across, zero)).astype(jnp.bfloat16)
            lowers.append(lower)
            if q < capacity:
                lower = jnp.where(level_ref[q] == 0, part_ref[q, k], lower)
            part_ref[q, k] = lower
        return lowers

    def absorb(group, before):
        for q in range(start, rows):
            facing = []
            for k in group:
                live, local = pick(q, k)
                faced = off_ref[local, MIRROR[k]] if k in INSIDE else near_off[k, local]
                facing.append(jnp.where(live, faced, zero))
            lowers = lower_blocks(q, group)
            schur = dot32(jnp.concatenate(lowers, axis=1), jnp.concatenate(facing, axis=0))
            rest_ref[q - start] = before(q) - schur

    absorb(INSIDE, lambda q: diag_ref[q].astype(jnp.float32))
    for side in SIDEWAYS:
        @pl.when(exists[side])
        def _():
            for kind in range(2):
                incoming(kind, side).wait_recv()
    absorb(SIDEWAYS, lambda q: rest_ref[q - start])
    for side in ALONG:
        @pl.when(exists[side])
        def _():
            incoming(1, side).wait_recv()
    for q in range(start, rows):
        for j, lower in enumerate(lower_blocks(q, ALONG)):
            lower_ref[q - start, j] = lower
    for side in ALONG:
        @pl.when(exists[side])
        def _():
            incoming(0, side).wait_recv()
            incoming(2, side).wait_recv()
    pivots = []
    for q in range(start, rows):
        facing = []
        for j, k in enumerate(ALONG):
            live, local = pick(q, k)
            facing.append(jnp.where(live, far_off[j, local], zero))
        lowers = [lower_ref[q - start, j] for j in range(len(ALONG))]
        schur = dot32(jnp.concatenate(lowers, axis=1), jnp.concatenate(facing, axis=0))
        pivots.append(rest_ref[q - start] - schur)
    second = inverses(pivots, False)
    for i in range(rows):
        if i < start:
            value = inv_ref[i]
        elif i < capacity:
            value = jnp.where(level_ref[i] == 0, inv_ref[i], second[i - start])
        else:
            value = second[i - start]
        pivot_ref[i] = value
    for side in range(REMOTE):
        @pl.when(exists[side])
        def _():
            for kind in range(3 if side in ALONG else 2):
                outgoing(kind, side).wait_send()


def store(pivot_ref, part_ref, pivot_hbm, factor_hbm, sems):
    rows = part_ref.shape[0]
    copies = [
        pltpu.make_async_copy(part_ref.at[i], factor_hbm.at[i], sems.at[i]) for i in range(rows)
    ] + [pltpu.make_async_copy(pivot_ref, pivot_hbm, sems.at[rows])]
    for copy in copies:
        copy.start()
    for copy in copies:
        copy.wait()


def solution(mesh):
    sizes = (mesh.shape["row"], mesh.shape["col"])

    def shards(diag_blocks, off_blocks, neighbors, levels):
        rows, slots, size, _ = off_blocks.shape
        capacity = 3 * rows // 4
        block = (size, size)
        hbm = pl.BlockSpec(memory_space=pltpu.HBM)
        vmem = pl.BlockSpec(memory_space=pltpu.VMEM)

        def shape(*lead):
            return jax.ShapeDtypeStruct(lead + block, jnp.bfloat16)

        def room(*lead):
            return pltpu.VMEM(lead + block, jnp.bfloat16)

        carried = pl.pallas_call(
            lambda *refs: exchange(sizes, capacity, *refs),
            name="exchange",
            out_shape=(shape(rows), shape(rows, slots)),
            in_specs=[hbm] * 4,
            out_specs=(vmem, vmem),
            scratch_shapes=[
                room(capacity),
                pltpu.VMEM((capacity,) + block, jnp.float32),
                room(capacity, 2),
                room(2, capacity),
                room(2, capacity),
                room(rows),
                room(rows, slots),
                pltpu.SMEM(neighbors.shape, jnp.int32),
                pltpu.SMEM(levels.shape, jnp.int32),
                room(2, capacity),
                room(2, capacity),
                pltpu.SemaphoreType.DMA((4,)),
                pltpu.SemaphoreType.DMA((3, REMOTE)),
                pltpu.SemaphoreType.DMA((3, REMOTE)),
                pltpu.SemaphoreType.REGULAR((len(SIDEWAYS),)),
            ],
            compiler_params=pltpu.CompilerParams(
                collective_id=0, has_side_effects=True, vmem_limit_bytes=VMEM_LIMIT
            ),
        )(*[pltpu.with_memory_space_constraint(x, pltpu.HBM) for x in (diag_blocks, off_blocks, neighbors, levels)])
        return pl.pallas_call(
            store,
            name="store",
            out_shape=(shape(rows), shape(rows, slots)),
            in_specs=[vmem] * 2,
            out_specs=(hbm, hbm),
            scratch_shapes=[pltpu.SemaphoreType.DMA((rows + 1,))],
            compiler_params=pltpu.CompilerParams(vmem_limit_bytes=VMEM_LIMIT),
        )(*carried)

    blocks = P(("row", "col"), None, None)
    wide = P(("row", "col"), None, None, None)
    in_specs = (blocks, wide, P(("row", "col"), None), P(("row", "col")))
    return jax.shard_map(shards, mesh=mesh, in_specs=in_specs, out_specs=(blocks, wide), check_vma=False)
```

```python
import jax
import jax.numpy as jnp
from jax import lax
from jax.experimental import pallas as pl
from jax.experimental.pallas import tpu as pltpu
from jax.sharding import PartitionSpec as P

NS_STEPS = 4
MIRROR = (1, 0, 3, 2, 5, 4)
MOVES = ((1, 0), (-1, 0), (0, 1), (0, -1))
REMOTE = len(MOVES)
MESH = pl.DeviceIdType.MESH
VMEM_LIMIT = 40 * 1024 * 1024
SIDEWAYS = (0, 1)
ALONG = (2, 3)
INSIDE = (4, 5)


def dot32(left, right):
    return jnp.dot(left, right, preferred_element_type=jnp.float32)


def split(value):
    high = value.astype(jnp.bfloat16)
    return high, (value - high.astype(jnp.float32)).astype(jnp.bfloat16)


def inverses(matrices, paired):
    size = matrices[0].shape[0]
    row_id = lax.broadcasted_iota(jnp.int32, (size, size), 0)
    col_id = lax.broadcasted_iota(jnp.int32, (size, size), 1)
    identity = (row_id == col_id).astype(jnp.float32)
    iterates = []
    for matrix in matrices:
        magnitude = jnp.abs(matrix)
        column_norm = jnp.max(jnp.sum(magnitude, axis=0, keepdims=True), axis=1, keepdims=True)
        row_norm = jnp.max(jnp.sum(magnitude, axis=1, keepdims=True), axis=0, keepdims=True)
        iterates.append(matrix.T * (1.0 / (column_norm * row_norm)))
    lefts = [matrix.astype(jnp.bfloat16) for matrix in matrices]
    if paired:
        lefts = [jnp.concatenate([left, left], axis=1) for left in lefts]
    for _ in range(NS_STEPS):
        halves = [split(iterate) if paired else (iterate.astype(jnp.bfloat16),) for iterate in iterates]
        rests = [
            (identity - dot32(left, jnp.concatenate(half, axis=0))).astype(jnp.bfloat16)
            for left, half in zip(lefts, halves)
        ]
        iterates = [
            iterate + dot32(jnp.concatenate(half, axis=1), jnp.concatenate([rest] * len(half), axis=0))
            for iterate, half, rest in zip(iterates, halves, rests)
        ]
    return [iterate.astype(jnp.bfloat16) for iterate in iterates]


def picker(named_ref, rows, capacity):
    def pick(q, k):
        named = named_ref[q, k]
        local = jnp.minimum(lax.rem(jnp.maximum(named, 0), rows), capacity - 1)
        return named >= 0, local

    return pick


def exchange(
    sizes, capacity, diag_hbm, off_hbm, named_hbm, level_hbm,
    pivot_ref, part_ref,
    inv_ref, rest_ref, lower_ref, far_off, far_inv, diag_ref, off_ref, named_ref, level_ref, near_off, near_inv, local_sem, send_sem, recv_sem, answer,
):
    rows, slots, size, _ = off_ref.shape
    start = rows - capacity
    zero = jnp.zeros((size, size), jnp.bfloat16)
    here = (lax.axis_index("row"), lax.axis_index("col"))
    there, exists = [], []
    for move in MOVES:
        target = tuple(here[axis] + move[axis] for axis in range(2))
        axis = 0 if move[0] != 0 else 1
        there.append(target)
        exists.append((target[axis] < sizes[axis]) if move[axis] > 0 else (target[axis] >= 0))

    barrier = pltpu.get_barrier_semaphore()
    odd = lax.rem(here[0], 2) == 1
    even = jnp.logical_not(odd)
    for side in range(REMOTE):
        @pl.when(exists[side] if side in ALONG else jnp.logical_and(exists[side], odd))
        def _():
            pl.semaphore_signal(barrier, inc=1, device_id=there[side], device_id_type=MESH)
    loads = [
        pltpu.make_async_copy(source, target, local_sem.at[i])
        for i, (source, target) in enumerate([
            (diag_hbm, diag_ref),
            (off_hbm, off_ref),
            (named_hbm, named_ref),
            (level_hbm, level_ref),
        ])
    ]
    for load in loads:
        load.start()
    pl.semaphore_wait(barrier, sum(
        (exists[side] if side in ALONG else jnp.logical_and(exists[side], even)).astype(jnp.int32)
        for side in range(REMOTE)
    ))

    pieces = (pl.ds(0, capacity - 1), pl.ds(0, capacity), pl.ds(capacity - 1, 1))

    def piece(kind, side):
        return pieces[1] if side in SIDEWAYS else pieces[kind]

    def landing(kind, side):
        if side in ALONG:
            target = (far_off, far_inv, far_off)[kind].at[side - ALONG[0]]
        else:
            target = (near_off, near_inv)[kind].at[side]
        return target.at[piece(kind, side)]

    def transfer(kind, source, side, arrives):
        return pltpu.make_async_remote_copy(
            src_ref=source,
            dst_ref=landing(kind, arrives),
            send_sem=send_sem.at[kind, side],
            recv_sem=recv_sem.at[kind, arrives],
            device_id=there[side],
            device_id_type=MESH,
        )

    def outgoing(kind, side):
        source = inv_ref if kind == 1 else off_hbm.at[piece(kind, side), side]
        return transfer(kind, source, side, MIRROR[side])

    def incoming(kind, side):
        return transfer(kind, landing(kind, side), side, side)

    for side in ALONG:
        @pl.when(exists[side])
        def _():
            outgoing(0, side).start()
    for side in SIDEWAYS:
        @pl.when(jnp.logical_and(exists[side], even))
        def _():
            pl.semaphore_signal(
                answer.at[MIRROR[side]], inc=1, device_id=there[side], device_id_type=MESH
            )
            outgoing(0, side).start()

        @pl.when(jnp.logical_and(exists[side], odd))
        def _():
            pl.semaphore_wait(answer.at[side], 1)
            outgoing(0, side).start()

    loads[0].wait()
    found = inverses([diag_ref[i].astype(jnp.float32) for i in range(capacity)], True)
    for i in range(capacity):
        inv_ref[i] = found[i]
    for side in ALONG:
        @pl.when(exists[side])
        def _():
            outgoing(1, side).start()
            outgoing(2, side).start()
    for side in SIDEWAYS:
        @pl.when(exists[side])
        def _():
            outgoing(1, side).start()

    for load in loads[1:]:
        load.wait()
    pick = picker(named_ref, rows, capacity)
    for i in range(capacity):
        upper = dot32(inv_ref[i], jnp.concatenate([off_ref[i, k] for k in range(slots)], axis=1))
        upper = upper.astype(jnp.bfloat16)
        for k in range(slots):
            part_ref[i, k] = jnp.where(
                named_ref[i, k] >= 0, upper[:, k * size : (k + 1) * size], zero
            )

    def lower_blocks(q, group):
        lowers = []
        for k in group:
            live, local = pick(q, k)
            if k in INSIDE:
                across = inv_ref[local]
            elif k in SIDEWAYS:
                across = near_inv[k, local]
            else:
                across = far_inv[k - ALONG[0], local]
            lower = dot32(off_ref[q, k], jnp.where(live, across, zero)).astype(jnp.bfloat16)
            lowers.append(lower)
            if q < capacity:
                lower = jnp.where(level_ref[q] == 0, part_ref[q, k], lower)
            part_ref[q, k] = lower
        return lowers

    def absorb(group, before):
        for q in range(start, rows):
            facing = []
            for k in group:
                live, local = pick(q, k)
                faced = off_ref[local, MIRROR[k]] if k in INSIDE else near_off[k, local]
                facing.append(jnp.where(live, faced, zero))
            lowers = lower_blocks(q, group)
            schur = dot32(jnp.concatenate(lowers, axis=1), jnp.concatenate(facing, axis=0))
            rest_ref[q - start] = before(q) - schur

    absorb(INSIDE, lambda q: diag_ref[q].astype(jnp.float32))
    for side in SIDEWAYS:
        @pl.when(exists[side])
        def _():
            for kind in range(2):
                incoming(kind, side).wait_recv()
    absorb(SIDEWAYS, lambda q: rest_ref[q - start])
    for side in ALONG:
        @pl.when(exists[side])
        def _():
            incoming(1, side).wait_recv()
    for q in range(start, rows):
        for j, lower in enumerate(lower_blocks(q, ALONG)):
            lower_ref[q - start, j] = lower
    for side in ALONG:
        @pl.when(exists[side])
        def _():
            incoming(0, side).wait_recv()
            incoming(2, side).wait_recv()
    pivots = []
    for q in range(start, rows):
        facing = []
        for j, k in enumerate(ALONG):
            live, local = pick(q, k)
            facing.append(jnp.where(live, far_off[j, local], zero))
        lowers = [lower_ref[q - start, j] for j in range(len(ALONG))]
        schur = dot32(jnp.concatenate(lowers, axis=1), jnp.concatenate(facing, axis=0))
        pivots.append(rest_ref[q - start] - schur)
    second = inverses(pivots, False)
    for i in range(rows):
        if i < start:
            value = inv_ref[i]
        elif i < capacity:
            value = jnp.where(level_ref[i] == 0, inv_ref[i], second[i - start])
        else:
            value = second[i - start]
        pivot_ref[i] = value
    for side in range(REMOTE):
        @pl.when(exists[side])
        def _():
            for kind in range(3 if side in ALONG else 2):
                outgoing(kind, side).wait_send()


def store(pivot_ref, part_ref, pivot_hbm, factor_hbm, sems):
    rows = part_ref.shape[0]
    copies = [
        pltpu.make_async_copy(part_ref.at[i], factor_hbm.at[i], sems.at[i]) for i in range(rows)
    ] + [pltpu.make_async_copy(pivot_ref, pivot_hbm, sems.at[rows])]
    for copy in copies:
        copy.start()
    for copy in copies:
        copy.wait()


def solution(mesh):
    sizes = (mesh.shape["row"], mesh.shape["col"])

    def shards(diag_blocks, off_blocks, neighbors, levels):
        rows, slots, size, _ = off_blocks.shape
        capacity = 3 * rows // 4
        block = (size, size)
        hbm = pl.BlockSpec(memory_space=pltpu.HBM)
        vmem = pl.BlockSpec(memory_space=pltpu.VMEM)

        def shape(*lead):
            return jax.ShapeDtypeStruct(lead + block, jnp.bfloat16)

        def room(*lead):
            return pltpu.VMEM(lead + block, jnp.bfloat16)

        carried = pl.pallas_call(
            lambda *refs: exchange(sizes, capacity, *refs),
            name="exchange",
            out_shape=(shape(rows), shape(rows, slots)),
            in_specs=[hbm] * 4,
            out_specs=(vmem, vmem),
            scratch_shapes=[
                room(capacity),
                pltpu.VMEM((capacity,) + block, jnp.float32),
                room(capacity, 2),
                room(2, capacity),
                room(2, capacity),
                room(rows),
                room(rows, slots),
                pltpu.SMEM(neighbors.shape, jnp.int32),
                pltpu.SMEM(levels.shape, jnp.int32),
                room(2, capacity),
                room(2, capacity),
                pltpu.SemaphoreType.DMA((4,)),
                pltpu.SemaphoreType.DMA((3, REMOTE)),
                pltpu.SemaphoreType.DMA((3, REMOTE)),
                pltpu.SemaphoreType.REGULAR((len(SIDEWAYS),)),
            ],
            compiler_params=pltpu.CompilerParams(
                collective_id=0, has_side_effects=True, vmem_limit_bytes=VMEM_LIMIT
            ),
        )(*[pltpu.with_memory_space_constraint(x, pltpu.HBM) for x in (diag_blocks, off_blocks, neighbors, levels)])
        return pl.pallas_call(
            store,
            name="store",
            out_shape=(shape(rows), shape(rows, slots)),
            in_specs=[vmem] * 2,
            out_specs=(hbm, hbm),
            scratch_shapes=[pltpu.SemaphoreType.DMA((rows + 1,))],
            compiler_params=pltpu.CompilerParams(vmem_limit_bytes=VMEM_LIMIT),
        )(*carried)

    blocks = P(("row", "col"), None, None)
    wide = P(("row", "col"), None, None, None)
    in_specs = (blocks, wide, P(("row", "col"), None), P(("row", "col")))
    return jax.shard_map(shards, mesh=mesh, in_specs=in_specs, out_specs=(blocks, wide), check_vma=False)
```

```python
import jax
import jax.numpy as jnp
from jax import lax
from jax.experimental import pallas as pl
from jax.experimental.pallas import tpu as pltpu
from jax.sharding import PartitionSpec as P

NS_STEPS = 4
MIRROR = (1, 0, 3, 2, 5, 4)
MOVES = ((1, 0), (-1, 0), (0, 1), (0, -1))
REMOTE = len(MOVES)
MESH = pl.DeviceIdType.MESH
VMEM_LIMIT = 40 * 1024 * 1024
SIDEWAYS = (0, 1)
ALONG = (2, 3)
INSIDE = (4, 5)


def dot32(left, right):
    return jnp.dot(left, right, preferred_element_type=jnp.float32)


def inverses(matrices):
    size = matrices[0].shape[0]
    row_id = lax.broadcasted_iota(jnp.int32, (size, size), 0)
    col_id = lax.broadcasted_iota(jnp.int32, (size, size), 1)
    identity = (row_id == col_id).astype(jnp.float32)
    iterates = []
    for matrix in matrices:
        magnitude = jnp.abs(matrix)
        column_norm = jnp.max(jnp.sum(magnitude, axis=0, keepdims=True), axis=1, keepdims=True)
        row_norm = jnp.max(jnp.sum(magnitude, axis=1, keepdims=True), axis=0, keepdims=True)
        iterates.append(matrix.T * (1.0 / (column_norm * row_norm)))
    lefts = [matrix.astype(jnp.bfloat16) for matrix in matrices]
    for _ in range(NS_STEPS):
        rounded = [iterate.astype(jnp.bfloat16) for iterate in iterates]
        rests = [(identity - dot32(left, x)).astype(jnp.bfloat16) for left, x in zip(lefts, rounded)]
        iterates = [iterate + dot32(x, rest) for iterate, x, rest in zip(iterates, rounded, rests)]
    return [iterate.astype(jnp.bfloat16) for iterate in iterates]


def picker(named_ref, rows, capacity):
    def pick(q, k):
        named = named_ref[q, k]
        local = jnp.minimum(lax.rem(jnp.maximum(named, 0), rows), capacity - 1)
        return named >= 0, local

    return pick


def exchange(
    sizes, capacity, diag_hbm, off_hbm, named_hbm, level_hbm,
    pivot_ref, part_ref,
    inv_ref, rest_ref, lower_ref, far_off, far_inv, diag_ref, off_ref, named_ref, level_ref, near_off, near_inv, local_sem, send_sem, recv_sem, answer,
):
    rows, slots, size, _ = off_ref.shape
    start = rows - capacity
    zero = jnp.zeros((size, size), jnp.bfloat16)
    here = (lax.axis_index("row"), lax.axis_index("col"))
    there, exists = [], []
    for move in MOVES:
        target = tuple(here[axis] + move[axis] for axis in range(2))
        axis = 0 if move[0] != 0 else 1
        there.append(target)
        exists.append((target[axis] < sizes[axis]) if move[axis] > 0 else (target[axis] >= 0))

    barrier = pltpu.get_barrier_semaphore()
    odd = lax.rem(here[0], 2) == 1
    even = jnp.logical_not(odd)
    for side in range(REMOTE):
        @pl.when(exists[side] if side in ALONG else jnp.logical_and(exists[side], odd))
        def _():
            pl.semaphore_signal(barrier, inc=1, device_id=there[side], device_id_type=MESH)
    loads = [
        pltpu.make_async_copy(source, target, local_sem.at[i])
        for i, (source, target) in enumerate([
            (diag_hbm, diag_ref),
            (off_hbm, off_ref),
            (named_hbm, named_ref),
            (level_hbm, level_ref),
        ])
    ]
    for load in loads:
        load.start()
    pl.semaphore_wait(barrier, sum(
        (exists[side] if side in ALONG else jnp.logical_and(exists[side], even)).astype(jnp.int32)
        for side in range(REMOTE)
    ))

    pieces = (pl.ds(0, capacity - 1), pl.ds(0, capacity), pl.ds(capacity - 1, 1))

    def piece(kind, side):
        return pieces[1] if side in SIDEWAYS else pieces[kind]

    def landing(kind, side):
        if side in ALONG:
            target = (far_off, far_inv, far_off)[kind].at[side - ALONG[0]]
        else:
            target = (near_off, near_inv)[kind].at[side]
        return target.at[piece(kind, side)]

    def transfer(kind, source, side, arrives):
        return pltpu.make_async_remote_copy(
            src_ref=source,
            dst_ref=landing(kind, arrives),
            send_sem=send_sem.at[kind, side],
            recv_sem=recv_sem.at[kind, arrives],
            device_id=there[side],
            device_id_type=MESH,
        )

    def outgoing(kind, side):
        source = inv_ref if kind == 1 else off_hbm.at[piece(kind, side), side]
        return transfer(kind, source, side, MIRROR[side])

    def incoming(kind, side):
        return transfer(kind, landing(kind, side), side, side)

    for side in ALONG:
        @pl.when(exists[side])
        def _():
            outgoing(0, side).start()
    for side in SIDEWAYS:
        @pl.when(jnp.logical_and(exists[side], even))
        def _():
            pl.semaphore_signal(
                answer.at[MIRROR[side]], inc=1, device_id=there[side], device_id_type=MESH
            )
            outgoing(0, side).start()

    loads[0].wait()
    found = inverses([diag_ref[i].astype(jnp.float32) for i in range(capacity)])
    for i in range(capacity):
        inv_ref[i] = found[i]
    for side in ALONG:
        @pl.when(exists[side])
        def _():
            outgoing(1, side).start()
            outgoing(2, side).start()
    for side in SIDEWAYS:
        @pl.when(jnp.logical_and(exists[side], even))
        def _():
            outgoing(1, side).start()

        @pl.when(jnp.logical_and(exists[side], odd))
        def _():
            pl.semaphore_wait(answer.at[side], 1)
            outgoing(0, side).start()
            outgoing(1, side).start()

    for load in loads[1:]:
        load.wait()
    pick = picker(named_ref, rows, capacity)
    for i in range(capacity):
        upper = dot32(inv_ref[i], jnp.concatenate([off_ref[i, k] for k in range(slots)], axis=1))
        upper = upper.astype(jnp.bfloat16)
        for k in range(slots):
            part_ref[i, k] = jnp.where(
                named_ref[i, k] >= 0, upper[:, k * size : (k + 1) * size], zero
            )

    def lower_blocks(q, group):
        lowers = []
        for k in group:
            live, local = pick(q, k)
            if k in INSIDE:
                across = inv_ref[local]
            elif k in SIDEWAYS:
                across = near_inv[k, local]
            else:
                across = far_inv[k - ALONG[0], local]
            lower = dot32(off_ref[q, k], jnp.where(live, across, zero)).astype(jnp.bfloat16)
            lowers.append(lower)
            if q < capacity:
                lower = jnp.where(level_ref[q] == 0, part_ref[q, k], lower)
            part_ref[q, k] = lower
        return lowers

    def absorb(group, before):
        for q in range(start, rows):
            facing = []
            for k in group:
                live, local = pick(q, k)
                faced = off_ref[local, MIRROR[k]] if k in INSIDE else near_off[k, local]
                facing.append(jnp.where(live, faced, zero))
            lowers = lower_blocks(q, group)
            schur = dot32(jnp.concatenate(lowers, axis=1), jnp.concatenate(facing, axis=0))
            rest_ref[q - start] = before(q) - schur

    absorb(INSIDE, lambda q: diag_ref[q].astype(jnp.float32))
    for side in SIDEWAYS:
        @pl.when(exists[side])
        def _():
            for kind in range(2):
                incoming(kind, side).wait_recv()
    absorb(SIDEWAYS, lambda q: rest_ref[q - start])
    for side in ALONG:
        @pl.when(exists[side])
        def _():
            incoming(1, side).wait_recv()
    for q in range(start, rows):
        for j, lower in enumerate(lower_blocks(q, ALONG)):
            lower_ref[q - start, j] = lower
    for side in ALONG:
        @pl.when(exists[side])
        def _():
            incoming(0, side).wait_recv()
            incoming(2, side).wait_recv()
    pivots = []
    for q in range(start, rows):
        facing = []
        for j, k in enumerate(ALONG):
            live, local = pick(q, k)
            facing.append(jnp.where(live, far_off[j, local], zero))
        lowers = [lower_ref[q - start, j] for j in range(len(ALONG))]
        schur = dot32(jnp.concatenate(lowers, axis=1), jnp.concatenate(facing, axis=0))
        pivots.append(rest_ref[q - start] - schur)
    second = inverses(pivots)
    for i in range(rows):
        if i < start:
            value = inv_ref[i]
        elif i < capacity:
            value = jnp.where(level_ref[i] == 0, inv_ref[i], second[i - start])
        else:
            value = second[i - start]
        pivot_ref[i] = value
    for side in range(REMOTE):
        @pl.when(exists[side])
        def _():
            for kind in range(3 if side in ALONG else 2):
                outgoing(kind, side).wait_send()


def store(pivot_ref, part_ref, pivot_hbm, factor_hbm, sems):
    rows = part_ref.shape[0]
    copies = [
        pltpu.make_async_copy(part_ref.at[i], factor_hbm.at[i], sems.at[i]) for i in range(rows)
    ] + [pltpu.make_async_copy(pivot_ref, pivot_hbm, sems.at[rows])]
    for copy in copies:
        copy.start()
    for copy in copies:
        copy.wait()


def solution(mesh):
    sizes = (mesh.shape["row"], mesh.shape["col"])

    def shards(diag_blocks, off_blocks, neighbors, levels):
        rows, slots, size, _ = off_blocks.shape
        capacity = 3 * rows // 4
        block = (size, size)
        hbm = pl.BlockSpec(memory_space=pltpu.HBM)
        vmem = pl.BlockSpec(memory_space=pltpu.VMEM)

        def shape(*lead):
            return jax.ShapeDtypeStruct(lead + block, jnp.bfloat16)

        def room(*lead):
            return pltpu.VMEM(lead + block, jnp.bfloat16)

        carried = pl.pallas_call(
            lambda *refs: exchange(sizes, capacity, *refs),
            name="exchange",
            out_shape=(shape(rows), shape(rows, slots)),
            in_specs=[hbm] * 4,
            out_specs=(vmem, vmem),
            scratch_shapes=[
                room(capacity),
                pltpu.VMEM((capacity,) + block, jnp.float32),
                room(capacity, 2),
                room(2, capacity),
                room(2, capacity),
                room(rows),
                room(rows, slots),
                pltpu.SMEM(neighbors.shape, jnp.int32),
                pltpu.SMEM(levels.shape, jnp.int32),
                room(2, capacity),
                room(2, capacity),
                pltpu.SemaphoreType.DMA((4,)),
                pltpu.SemaphoreType.DMA((3, REMOTE)),
                pltpu.SemaphoreType.DMA((3, REMOTE)),
                pltpu.SemaphoreType.REGULAR((len(SIDEWAYS),)),
            ],
            compiler_params=pltpu.CompilerParams(
                collective_id=0, has_side_effects=True, vmem_limit_bytes=VMEM_LIMIT
            ),
        )(*[pltpu.with_memory_space_constraint(x, pltpu.HBM) for x in (diag_blocks, off_blocks, neighbors, levels)])
        return pl.pallas_call(
            store,
            name="store",
            out_shape=(shape(rows), shape(rows, slots)),
            in_specs=[vmem] * 2,
            out_specs=(hbm, hbm),
            scratch_shapes=[pltpu.SemaphoreType.DMA((rows + 1,))],
            compiler_params=pltpu.CompilerParams(vmem_limit_bytes=VMEM_LIMIT),
        )(*carried)

    blocks = P(("row", "col"), None, None)
    wide = P(("row", "col"), None, None, None)
    in_specs = (blocks, wide, P(("row", "col"), None), P(("row", "col")))
    return jax.shard_map(shards, mesh=mesh, in_specs=in_specs, out_specs=(blocks, wide), check_vma=False)
```

```python
import jax
import jax.numpy as jnp
from jax import lax
from jax.experimental import pallas as pl
from jax.experimental.pallas import tpu as pltpu
from jax.sharding import PartitionSpec as P

NS_STEPS = 4
MIRROR = (1, 0, 3, 2, 5, 4)
MOVES = ((1, 0), (-1, 0), (0, 1), (0, -1))
REMOTE = len(MOVES)
MESH = pl.DeviceIdType.MESH
VMEM_LIMIT = 40 * 1024 * 1024
SIDEWAYS = (0, 1)
ALONG = (2, 3)
INSIDE = (4, 5)


def dot32(left, right):
    return jnp.dot(left, right, preferred_element_type=jnp.float32)


def inverses(matrices):
    size = matrices[0].shape[0]
    row_id = lax.broadcasted_iota(jnp.int32, (size, size), 0)
    col_id = lax.broadcasted_iota(jnp.int32, (size, size), 1)
    identity = (row_id == col_id).astype(jnp.float32)
    iterates = []
    for matrix in matrices:
        magnitude = jnp.abs(matrix)
        column_norm = jnp.max(jnp.sum(magnitude, axis=0, keepdims=True), axis=1, keepdims=True)
        row_norm = jnp.max(jnp.sum(magnitude, axis=1, keepdims=True), axis=0, keepdims=True)
        iterates.append(matrix.T * (1.0 / (column_norm * row_norm)))
    lefts = [matrix.astype(jnp.bfloat16) for matrix in matrices]
    for _ in range(NS_STEPS):
        rounded = [iterate.astype(jnp.bfloat16) for iterate in iterates]
        rests = [(identity - dot32(left, x)).astype(jnp.bfloat16) for left, x in zip(lefts, rounded)]
        iterates = [iterate + dot32(x, rest) for iterate, x, rest in zip(iterates, rounded, rests)]
    return [iterate.astype(jnp.bfloat16) for iterate in iterates]


def picker(named_ref, rows, capacity):
    def pick(q, k):
        named = named_ref[q, k]
        local = jnp.minimum(lax.rem(jnp.maximum(named, 0), rows), capacity - 1)
        return named >= 0, local

    return pick


def exchange(
    sizes, capacity, diag_hbm, off_hbm, named_hbm, level_hbm,
    pivot_ref, part_ref,
    inv_ref, rest_ref, lower_ref, far_off, far_inv, diag_ref, off_ref, named_ref, level_ref, near_off, near_inv, local_sem, send_sem, recv_sem, answer,
):
    rows, slots, size, _ = off_ref.shape
    start = rows - capacity
    zero = jnp.zeros((size, size), jnp.bfloat16)
    here = (lax.axis_index("row"), lax.axis_index("col"))
    there, exists = [], []
    for move in MOVES:
        target = tuple(here[axis] + move[axis] for axis in range(2))
        axis = 0 if move[0] != 0 else 1
        there.append(target)
        exists.append((target[axis] < sizes[axis]) if move[axis] > 0 else (target[axis] >= 0))

    barrier = pltpu.get_barrier_semaphore()
    odd = lax.rem(here[0], 2) == 1
    even = jnp.logical_not(odd)
    for side in range(REMOTE):
        @pl.when(exists[side] if side in ALONG else jnp.logical_and(exists[side], odd))
        def _():
            pl.semaphore_signal(barrier, inc=1, device_id=there[side], device_id_type=MESH)
    loads = [
        pltpu.make_async_copy(source, target, local_sem.at[i])
        for i, (source, target) in enumerate([
            (diag_hbm, diag_ref),
            (off_hbm, off_ref),
            (named_hbm, named_ref),
            (level_hbm, level_ref),
        ])
    ]
    loads[0].start()
    pl.semaphore_wait(barrier, sum(
        (exists[side] if side in ALONG else jnp.logical_and(exists[side], even)).astype(jnp.int32)
        for side in range(REMOTE)
    ))

    pieces = (pl.ds(0, capacity - 1), pl.ds(0, capacity), pl.ds(capacity - 1, 1))

    def piece(kind, side):
        return pieces[1] if side in SIDEWAYS else pieces[kind]

    def landing(kind, side):
        if side in ALONG:
            target = (far_off, far_inv, far_off)[kind].at[side - ALONG[0]]
        else:
            target = (near_off, near_inv)[kind].at[side]
        return target.at[piece(kind, side)]

    def transfer(kind, source, side, arrives):
        return pltpu.make_async_remote_copy(
            src_ref=source,
            dst_ref=landing(kind, arrives),
            send_sem=send_sem.at[kind, side],
            recv_sem=recv_sem.at[kind, arrives],
            device_id=there[side],
            device_id_type=MESH,
        )

    def outgoing(kind, side):
        source = inv_ref if kind == 1 else off_hbm.at[piece(kind, side), side]
        return transfer(kind, source, side, MIRROR[side])

    def incoming(kind, side):
        return transfer(kind, landing(kind, side), side, side)

    for side in ALONG:
        @pl.when(exists[side])
        def _():
            outgoing(0, side).start()
    for side in SIDEWAYS:
        @pl.when(jnp.logical_and(exists[side], even))
        def _():
            pl.semaphore_signal(
                answer.at[MIRROR[side]], inc=1, device_id=there[side], device_id_type=MESH
            )
            outgoing(0, side).start()

    for load in loads[1:]:
        load.start()
    loads[0].wait()
    found = inverses([diag_ref[i].astype(jnp.float32) for i in range(capacity)])
    for i in range(capacity):
        inv_ref[i] = found[i]
    for side in ALONG:
        @pl.when(exists[side])
        def _():
            outgoing(1, side).start()
            outgoing(2, side).start()
    for side in SIDEWAYS:
        @pl.when(jnp.logical_and(exists[side], even))
        def _():
            outgoing(1, side).start()

        @pl.when(jnp.logical_and(exists[side], odd))
        def _():
            pl.semaphore_wait(answer.at[side], 1)
            outgoing(0, side).start()
            outgoing(1, side).start()

    for load in loads[1:]:
        load.wait()
    pick = picker(named_ref, rows, capacity)
    for i in range(capacity):
        upper = dot32(inv_ref[i], jnp.concatenate([off_ref[i, k] for k in range(slots)], axis=1))
        upper = upper.astype(jnp.bfloat16)
        for k in range(slots):
            part_ref[i, k] = jnp.where(
                named_ref[i, k] >= 0, upper[:, k * size : (k + 1) * size], zero
            )

    def lower_blocks(q, group):
        lowers = []
        for k in group:
            live, local = pick(q, k)
            if k in INSIDE:
                across = inv_ref[local]
            elif k in SIDEWAYS:
                across = near_inv[k, local]
            else:
                across = far_inv[k - ALONG[0], local]
            lower = dot32(off_ref[q, k], jnp.where(live, across, zero)).astype(jnp.bfloat16)
            lowers.append(lower)
            if q < capacity:
                lower = jnp.where(level_ref[q] == 0, part_ref[q, k], lower)
            part_ref[q, k] = lower
        return lowers

    def absorb(group, before):
        for q in range(start, rows):
            facing = []
            for k in group:
                live, local = pick(q, k)
                faced = off_ref[local, MIRROR[k]] if k in INSIDE else near_off[k, local]
                facing.append(jnp.where(live, faced, zero))
            lowers = lower_blocks(q, group)
            schur = dot32(jnp.concatenate(lowers, axis=1), jnp.concatenate(facing, axis=0))
            rest_ref[q - start] = before(q) - schur

    absorb(INSIDE, lambda q: diag_ref[q].astype(jnp.float32))
    for side in SIDEWAYS:
        @pl.when(exists[side])
        def _():
            for kind in range(2):
                incoming(kind, side).wait_recv()
    absorb(SIDEWAYS, lambda q: rest_ref[q - start])
    for side in ALONG:
        @pl.when(exists[side])
        def _():
            incoming(1, side).wait_recv()
    for q in range(start, rows):
        for j, lower in enumerate(lower_blocks(q, ALONG)):
            lower_ref[q - start, j] = lower
    for side in ALONG:
        @pl.when(exists[side])
        def _():
            incoming(0, side).wait_recv()
            incoming(2, side).wait_recv()
    pivots = []
    for q in range(start, rows):
        facing = []
        for j, k in enumerate(ALONG):
            live, local = pick(q, k)
            facing.append(jnp.where(live, far_off[j, local], zero))
        lowers = [lower_ref[q - start, j] for j in range(len(ALONG))]
        schur = dot32(jnp.concatenate(lowers, axis=1), jnp.concatenate(facing, axis=0))
        pivots.append(rest_ref[q - start] - schur)
    second = inverses(pivots)
    for i in range(rows):
        if i < start:
            value = inv_ref[i]
        elif i < capacity:
            value = jnp.where(level_ref[i] == 0, inv_ref[i], second[i - start])
        else:
            value = second[i - start]
        pivot_ref[i] = value
    for side in range(REMOTE):
        @pl.when(exists[side])
        def _():
            for kind in range(3 if side in ALONG else 2):
                outgoing(kind, side).wait_send()


def store(pivot_ref, part_ref, pivot_hbm, factor_hbm, sems):
    rows = part_ref.shape[0]
    copies = [
        pltpu.make_async_copy(part_ref.at[i], factor_hbm.at[i], sems.at[i]) for i in range(rows)
    ] + [pltpu.make_async_copy(pivot_ref, pivot_hbm, sems.at[rows])]
    for copy in copies:
        copy.start()
    for copy in copies:
        copy.wait()


def solution(mesh):
    sizes = (mesh.shape["row"], mesh.shape["col"])

    def shards(diag_blocks, off_blocks, neighbors, levels):
        rows, slots, size, _ = off_blocks.shape
        capacity = 3 * rows // 4
        block = (size, size)
        hbm = pl.BlockSpec(memory_space=pltpu.HBM)
        vmem = pl.BlockSpec(memory_space=pltpu.VMEM)

        def shape(*lead):
            return jax.ShapeDtypeStruct(lead + block, jnp.bfloat16)

        def room(*lead):
            return pltpu.VMEM(lead + block, jnp.bfloat16)

        carried = pl.pallas_call(
            lambda *refs: exchange(sizes, capacity, *refs),
            name="exchange",
            out_shape=(shape(rows), shape(rows, slots)),
            in_specs=[hbm] * 4,
            out_specs=(vmem, vmem),
            scratch_shapes=[
                room(capacity),
                pltpu.VMEM((capacity,) + block, jnp.float32),
                room(capacity, 2),
                room(2, capacity),
                room(2, capacity),
                room(rows),
                room(rows, slots),
                pltpu.SMEM(neighbors.shape, jnp.int32),
                pltpu.SMEM(levels.shape, jnp.int32),
                room(2, capacity),
                room(2, capacity),
                pltpu.SemaphoreType.DMA((4,)),
                pltpu.SemaphoreType.DMA((3, REMOTE)),
                pltpu.SemaphoreType.DMA((3, REMOTE)),
                pltpu.SemaphoreType.REGULAR((len(SIDEWAYS),)),
            ],
            compiler_params=pltpu.CompilerParams(
                collective_id=0, has_side_effects=True, vmem_limit_bytes=VMEM_LIMIT
            ),
        )(*[pltpu.with_memory_space_constraint(x, pltpu.HBM) for x in (diag_blocks, off_blocks, neighbors, levels)])
        return pl.pallas_call(
            store,
            name="store",
            out_shape=(shape(rows), shape(rows, slots)),
            in_specs=[vmem] * 2,
            out_specs=(hbm, hbm),
            scratch_shapes=[pltpu.SemaphoreType.DMA((rows + 1,))],
            compiler_params=pltpu.CompilerParams(vmem_limit_bytes=VMEM_LIMIT),
        )(*carried)

    blocks = P(("row", "col"), None, None)
    wide = P(("row", "col"), None, None, None)
    in_specs = (blocks, wide, P(("row", "col"), None), P(("row", "col")))
    return jax.shard_map(shards, mesh=mesh, in_specs=in_specs, out_specs=(blocks, wide), check_vma=False)
```
